256 devices in a mesh: img: 64 (over x, z, y_lo), txt: 4 (over y_hi, core).
Axes of the slice: x: 4, y: 4 (y_hi: 2, y_lo: 2; y = y_hi * 2 + y_lo), z: 8, core: 2. Of those that a mesh axis runs over, the one named last changes fastest.
Arguments:
- image_tokens: bfloat16 [32768, 256], P(('img', 'txt')), may hold values from -6 to 6
- prompt_tokens: bfloat16 [6144, 256], P(('txt', 'img')), may hold values from -6 to 6
- category_ids: int32 [6144], P(('txt', 'img')), may hold values from 0 to 383, as said below
- prompt_valid: int32 [6144], P(('txt', 'img')), may hold values from 0 to 1, as said below
- image_gain: float32 [256], replicated, may hold values from 0.5 to 1.5
- prompt_gain: float32 [256], replicated, may hold values from 0.5 to 1.5
- query_weight: bfloat16 [256, 1024], replicated, may hold values from -1.7 to 1.7
- key_weight: bfloat16 [256, 1024], replicated, may hold values from -1.7 to 1.7
- image_value_weight: bfloat16 [256, 1024], replicated, may hold values from -0.375 to 0.375
- prompt_value_weight: bfloat16 [256, 1024], replicated, may hold values from -0.375 to 0.375
- image_out_weight: bfloat16 [1024, 256], replicated, may hold values from -0.1875 to 0.1875
- prompt_out_weight: bfloat16 [1024, 256], replicated, may hold values from -0.1875 to 0.1875
- image_layer_scale: float32 [256], replicated, may hold values from 1 to 4
- prompt_layer_scale: float32 [256], replicated, may hold values from 1 to 4
Outputs:
- joined_image: bfloat16 [32768, 256], P(('img', 'txt'))
- joined_prompt: bfloat16 [6144, 256], P(('txt', 'img'))
- category_embed: float32 [384, 256], replicated
The draws below stay inside these ranges and needn't reach their ends.
Inputs may be any that keep to these rules, and one draw needn't show every extreme that they name: `category_ids`: along the prompt the ids never fall; each of the 384 categories holds between 4 and 28 consecutive tokens. `prompt_valid`: within each category the tokens marked 1 come first, and at least one token is marked 1.
All inputs are finite; a program needn't handle non-finite values.
Results may differ from the reference program's by a relative error of at most 0.009.
The reference program's roundings to bfloat16 on the way count: a program that leaves them out, or rounds other values in their place, can miss the bound.
Values may be sent and summed in bfloat16 or wider, within the bound.
No kernel may reach another device: no remote copies, remote signals or barrier semaphores. Data moves between devices by JAX's collectives and lax.ppermute only.
A program may use at most 128 MiB of HBM per device.

```python
import math
import jax
import jax.numpy as jnp
from jax import lax

D = 256
HEADS = 4
HD = 256
NI = 32768
NT = 6144
IMG_BLK = 512
TXT_BLK = 1536
CATS = 384
N_IMG = 64
N_TXT = 4


def category_starts(key):
    jitter = jax.random.randint(jax.random.fold_in(key, 11), (CATS - 1,), -6, 7)
    return jnp.arange(1, CATS, dtype=jnp.int32) * 16 + jitter.astype(jnp.int32)


def category_of(starts):
    positions = jnp.arange(NT, dtype=jnp.int32)
    return jnp.sum((positions[:, None] >= starts[None, :]).astype(jnp.int32), axis=1).astype(jnp.int32)


def draw_category_ids(key, part):
    return category_of(category_starts(key))


def draw_prompt_valid(key, part):
    starts = category_starts(key)
    lower = jnp.concatenate([jnp.zeros((1,), jnp.int32), starts])
    upper = jnp.concatenate([starts, jnp.full((1,), NT, jnp.int32)])
    kept = jax.random.randint(jax.random.fold_in(key, 23), (CATS,), 1, upper - lower + 1)
    owner = category_of(starts)
    offset = jnp.arange(NT, dtype=jnp.int32) - lower[owner]
    return (offset < kept[owner]).astype(jnp.int32)


def score_weight(key, salt):
    spread = 1.25 / math.sqrt(D)
    base = jnp.clip(jax.random.normal(jax.random.fold_in(key, salt), (D, HEADS * HD), jnp.float32), -6.0, 6.0) * spread
    return base.astype(jnp.bfloat16)


def draw_query_weight(key, part):
    return score_weight(key, 51)


def draw_key_weight(key, part):
    return score_weight(key, 52)


def shard_levels(rng, shape, split, low, largest):
    level, own = 1.0, jax.random.fold_in(rng, 6)
    for position, blocks in split:
        steps = jnp.exp(jax.random.uniform(jax.random.fold_in(own, position), (blocks,), jnp.float32, low / len(split), largest / len(split)))
        level = level * jnp.repeat(steps, shape[position] // blocks).reshape([-1 if axis == position else 1 for axis in range(len(shape))])
    return level


def gaussian(own_key, extent, deviation, reach, pieces=(), kind=jnp.bfloat16):
    entries = jax.random.normal(own_key, extent, jnp.float32) * deviation
    if len(pieces) > 0:
        entries = shard_levels(own_key, extent, pieces, -0.22, 0.18) * entries
    return jnp.clip(entries, min=-reach, max=reach).astype(kind)


def setup_inputs(seed: int = 0) -> dict:
    arg_keys = jax.random.split(jax.random.key(seed), 15)
    return {
        "image_tokens": gaussian(arg_keys[0], (NI, D), 1.0, 6.0, ((0, 256),)),
        "prompt_tokens": gaussian(arg_keys[1], (NT, D), 1.0, 6.0, ((0, 256),)),
        "category_ids": draw_category_ids(jax.random.fold_in(arg_keys[14], 71), 0),
        "prompt_valid": draw_prompt_valid(jax.random.fold_in(arg_keys[14], 71), 0),
        "image_gain": jnp.clip(1.0 + 0.1 * jax.random.normal(arg_keys[4], (D,), jnp.float32), 0.5, 1.5),
        "prompt_gain": jnp.clip(1.0 + 0.1 * jax.random.normal(arg_keys[5], (D,), jnp.float32), 0.5, 1.5),
        "query_weight": draw_query_weight(jax.random.fold_in(arg_keys[14], 71), 0),
        "key_weight": draw_key_weight(jax.random.fold_in(arg_keys[14], 71), 0),
        "image_value_weight": gaussian(arg_keys[8], (D, HEADS * HD), D ** -0.5, 0.375),
        "prompt_value_weight": gaussian(arg_keys[9], (D, HEADS * HD), D ** -0.5, 0.375),
        "image_out_weight": gaussian(arg_keys[10], (HEADS * HD, D), (HEADS * HD) ** -0.5, 0.1875),
        "prompt_out_weight": gaussian(arg_keys[11], (HEADS * HD, D), (HEADS * HD) ** -0.5, 0.1875),
        "image_layer_scale": jnp.clip(jnp.exp(jax.random.uniform(arg_keys[12], (D,), jnp.float32, math.log(1.0), math.log(4.0))), 1.0, 4.0),
        "prompt_layer_scale": jnp.clip(jnp.exp(jax.random.uniform(arg_keys[13], (D,), jnp.float32, math.log(1.0), math.log(4.0))), 1.0, 4.0),
    }


EPSILON = 1e-05
MASKED = -1e+30

def normalize(tokens_in, gain_row):
    values = tokens_in.astype(jnp.float32)
    average = lax.optimization_barrier(jnp.mean(values, axis=-1, keepdims=True))
    centered = values - average
    variance = lax.optimization_barrier(jnp.mean(centered * centered, axis=-1, keepdims=True))
    return (centered * lax.rsqrt(variance + EPSILON) * gain_row).astype(jnp.bfloat16)

def reference(image_tokens, prompt_tokens, category_ids, prompt_valid, image_gain, prompt_gain, query_weight, key_weight, image_value_weight, prompt_value_weight, image_out_weight, prompt_out_weight, image_layer_scale, prompt_layer_scale):
    embed_width = query_weight.shape[1]
    head_count = embed_width // HD
    image_normed = normalize(image_tokens, image_gain)
    prompt_normed = normalize(prompt_tokens, prompt_gain)
    queries = jnp.dot(image_normed.astype(jnp.float32), query_weight.astype(jnp.float32), preferred_element_type=jnp.float32).astype(jnp.bfloat16)
    image_values = jnp.dot(image_normed.astype(jnp.float32), image_value_weight.astype(jnp.float32), preferred_element_type=jnp.float32).astype(jnp.bfloat16)
    prompt_keys = jnp.dot(prompt_normed.astype(jnp.float32), key_weight.astype(jnp.float32), preferred_element_type=jnp.float32).astype(jnp.bfloat16)
    prompt_values = jnp.dot(prompt_normed.astype(jnp.float32), prompt_value_weight.astype(jnp.float32), preferred_element_type=jnp.float32).astype(jnp.bfloat16)
    key_heads = prompt_keys.reshape(NT, head_count, HD).astype(jnp.float32)
    value_blocks = prompt_values.reshape(N_TXT, TXT_BLK, head_count, HD).astype(jnp.float32)
    query_blocks = queries.reshape(N_IMG, IMG_BLK, head_count, HD)
    image_value_blocks = image_values.reshape(N_IMG, IMG_BLK, head_count, HD)
    is_valid = (prompt_valid > 0)[None, None, :]
    image_out = image_out_weight.astype(jnp.float32)

    def block_scores(query_block):
        return jnp.einsum('ihd,thd->hit', query_block.astype(jnp.float32), key_heads) / math.sqrt(HD)

    def first_pass(carry, query_block):
        col_top, col_sum = carry
        scores = block_scores(query_block)
        masked = jnp.where(is_valid, scores, MASKED)
        row_top = lax.optimization_barrier(jnp.max(masked, axis=2))
        row_exp = jnp.where(is_valid, jnp.exp(masked - row_top[:, :, None]), 0.0)
        row_sum = lax.optimization_barrier(jnp.sum(row_exp, axis=2))
        rounded = lax.optimization_barrier(row_exp.astype(jnp.bfloat16)).astype(jnp.float32)
        split_weights = rounded.reshape(head_count, IMG_BLK, N_TXT, TXT_BLK)
        image_parts = jnp.einsum('hibt,bthd->bihd', split_weights, value_blocks) / row_sum.T[None, :, :, None]
        image_parts = image_parts.reshape(N_TXT, IMG_BLK, embed_width).astype(jnp.bfloat16)
        image_delta = jnp.einsum('bie,ef->if', image_parts.astype(jnp.float32), image_out)
        new_top = jnp.maximum(col_top, lax.optimization_barrier(jnp.max(scores, axis=1)))
        new_sum = col_sum * jnp.exp(col_top - new_top) + lax.optimization_barrier(jnp.sum(jnp.exp(scores - new_top[:, None, :]), axis=1))
        return ((new_top, new_sum), image_delta)
    start_carry = (jnp.full((head_count, NT), MASKED, dtype=jnp.float32), jnp.zeros((head_count, NT), dtype=jnp.float32))
    scanned = lax.scan(first_pass, start_carry, query_blocks)
    col_top, col_sum = scanned[0]
    image_delta = scanned[1].reshape(NI, D)
    joined_image = (image_tokens.astype(jnp.float32) + image_layer_scale * image_delta).astype(jnp.bfloat16)

    def second_pass(prompt_delta, blocks):
        query_block, value_block = blocks
        scores = block_scores(query_block)
        col_exp = jnp.exp(scores - col_top[:, None, :])
        rounded = lax.optimization_barrier(col_exp.astype(jnp.bfloat16)).astype(jnp.float32)
        prompt_part = jnp.einsum('hit,ihd->thd', rounded, value_block.astype(jnp.float32)) / col_sum.T[:, :, None]
        prompt_part = prompt_part.reshape(NT, embed_width).astype(jnp.bfloat16)
        return (prompt_delta + jnp.dot(prompt_part.astype(jnp.float32), prompt_out_weight.astype(jnp.float32), preferred_element_type=jnp.float32), None)
    prompt_delta = lax.scan(second_pass, jnp.zeros((NT, D), dtype=jnp.float32), (query_blocks, image_value_blocks))[0]
    prompt_joined = prompt_tokens.astype(jnp.float32) + prompt_layer_scale * prompt_delta
    joined_prompt = prompt_joined.astype(jnp.bfloat16)
    members = jnp.logical_and(category_ids[None, :] == jnp.arange(CATS, dtype=jnp.int32)[:, None], prompt_valid[None, :] > 0).astype(jnp.float32)
    category_sum = jnp.dot(members, prompt_joined, precision=lax.Precision.HIGHEST)
    category_embed = category_sum / lax.optimization_barrier(jnp.sum(members, axis=1))[:, None]
    return (joined_image, joined_prompt, category_embed)
```

```python
import functools
import math

import jax
import jax.numpy as jnp
from jax import lax
from jax.experimental import pallas as pl
from jax.experimental.pallas import tpu as pltpu
from jax.sharding import Mesh
from jax.sharding import PartitionSpec as P

HD = 256
CHUNK = 256
EPSILON = 1e-05
MASKED = -1e30
ALL = ("x", "z", "yl", "yh", "c")
PROMPT_ORDER = ("yh", "c", "x", "z", "yl")
PLANE = ("x", "z")
COLUMN = ("yl", "yh", "c")
BF = jnp.bfloat16
F32 = jnp.float32


def swap(parts, axes):
    return lax.all_to_all(parts, axes, split_axis=0, concat_axis=0, tiled=True)


def spread(shard, axes):
    copies = jnp.broadcast_to(shard, (lax.axis_size(axes), *shard.shape))
    return swap(copies, axes)


def normed(tokens, gain_row):
    values = tokens.astype(F32)
    centered = values - jnp.mean(values, axis=-1, keepdims=True)
    variance = jnp.mean(centered * centered, axis=-1, keepdims=True)
    return (centered * lax.rsqrt(variance + EPSILON) * gain_row).astype(BF)


def dot(left, right):
    return jnp.dot(left, right, preferred_element_type=F32)


def dot_nt(left, right):
    return lax.dot_general(left, right, (((1,), (1,)), ((), ())), preferred_element_type=F32)


def image_kernel(tokens, gain, query_w, value_wt, queries, values_t, held):
    @pl.when(pl.program_id(0) == 0)
    def _():
        held[...] = normed(tokens[...], gain[...])

    factor = math.log2(math.e) / math.sqrt(HD)
    queries[...] = (dot(held[...], query_w[...]) * factor).astype(BF)
    values_t[...] = dot_nt(value_wt[...], held[...]).astype(BF)


def attend(reduced, kept, values_t, bias, out_t, lse, head):
    for at in range(0, kept.shape[0], CHUNK):
        scores = dot_nt(reduced, kept[at : at + CHUNK])
        if bias is not None:
            scores = scores + bias
        top = jnp.max(scores, axis=0, keepdims=True)
        weights = jnp.exp2(scores - top)
        total = jnp.sum(weights, axis=0, keepdims=True)
        numer = dot(values_t, weights.astype(BF))
        out_t[:, at : at + CHUNK] = numer * (1.0 / total)
        stat = top + jnp.log2(total)
        rows = kept.shape[0] // 128
        for k in range(CHUNK // 128):
            lse[pl.ds(head * rows + at // 128 + k, 1), :] = stat[:, k * 128 : (k + 1) * 128]


def column_kernel(tokens, gain, key_w, queries, values_t, keys, out_t, lse, held):
    head = pl.program_id(0)

    @pl.when(head == 0)
    def _():
        held[...] = normed(tokens[...], gain[...])

    key = dot(held[...], key_w[...]).astype(BF)
    keys[...] = key
    attend(queries[...], key, values_t[...], None, out_t, lse, head)


def row_kernel(tokens, gain, value_wt, keys, queries, bias, out_t, lse, held):
    head = pl.program_id(0)

    @pl.when(head == 0)
    def _():
        held[...] = normed(tokens[...], gain[...])

    values_t = dot_nt(value_wt[...], held[...]).astype(BF)
    attend(keys[...], queries[...], values_t, bias[...], out_t, lse, head)


def projected(lse_all, lse, out_t, out_wt):
    gathered = lse_all[...]
    highest = jnp.max(gathered, axis=0)
    whole = highest + jnp.log2(jnp.sum(jnp.exp2(gathered - highest[None]), axis=0))
    share = jnp.exp2(lse[...] - whole)
    heads = out_t.shape[0] // HD
    rows = share.shape[0] // heads
    total = None
    for head in range(heads):
        line = jnp.concatenate(
            [share[head * rows + k : head * rows + k + 1] for k in range(rows)], axis=1
        )
        block = slice(head * HD, (head + 1) * HD)
        part = (out_t[block, :] * line).astype(BF)
        term = dot(out_wt[:, block], part)
        total = term if total is None else total + term
    return total.T.astype(BF)


def image_out_kernel(lse_all, lse, out_t, out_wt, sent):
    sent[...] = projected(lse_all, lse, out_t, out_wt)


def members_of(codes, first, count):
    wanted = 2 * (first + lax.broadcasted_iota(jnp.int32, (count, codes.shape[1]), 0)) + 1
    return jnp.where(codes == wanted, 1.0, 0.0).astype(BF)


def prompt_out_kernel(lse_all, lse, out_t, out_wt, codes, sent, sums):
    contribution = projected(lse_all, lse, out_t, out_wt)
    sent[...] = contribution
    groups = sums.shape[0] // 2
    rows = sums.shape[1]
    gathered = dot(members_of(codes[...], 0, groups * rows), contribution).astype(BF)
    for group in range(groups):
        for side in range(2):
            sums[2 * group + side] = gathered[
                group * rows : (group + 1) * rows, side * 128 : (side + 1) * 128
            ]


def category_kernel(place, arrived, codes, tokens, scale, out):
    rows = arrived.shape[1]
    group, side = place[0], place[1]
    members = members_of(codes[...], group * rows, rows)
    base = dot(members, tokens[...])
    wide = jnp.where(side == 0, base[:, :128], base[:, 128:])
    factor = jnp.where(side == 0, scale[:, :128], scale[:, 128:])
    out[0] = wide + factor * jnp.sum(arrived[...].astype(F32), axis=0)
    tally = jnp.sum(members.astype(F32), axis=1, keepdims=True)
    out[1] = jnp.broadcast_to(tally, out.shape[1:])


def block(shape, index):
    return pl.BlockSpec(shape, index)


def whole(array):
    rank = len(array.shape)
    return pl.BlockSpec(array.shape, lambda h: (0,) * rank)


def shaped(shape, dtype):
    return jax.ShapeDtypeStruct(shape, dtype)


def cost(flops, moved, exps=0):
    return pl.CostEstimate(flops=flops, bytes_accessed=moved, transcendentals=exps)


PARAMS = dict(dimension_semantics=("arbitrary",), vmem_limit_bytes=40 * 2**20)


def on_device(
    image_tokens,
    prompt_tokens,
    category_ids,
    prompt_valid,
    image_gain,
    prompt_gain,
    query_weight,
    key_weight,
    image_value_weight,
    prompt_value_weight,
    image_out_weight,
    prompt_out_weight,
    image_layer_scale,
    prompt_layer_scale,
):
    width = query_weight.shape[1]
    heads = width // HD
    depth = image_tokens.shape[1]
    planes = lax.axis_size(PLANE)
    columns = lax.axis_size(COLUMN)
    own_prompts = prompt_tokens.shape[0]
    own_images = image_tokens.shape[0]
    images = own_images * columns
    prompts = own_prompts * planes
    categories = prompts * columns // 16

    code = (2 * category_ids + prompt_valid).reshape(1, own_prompts)
    code = jnp.pad(code, ((0, 0), (0, 128 - own_prompts)))
    prompt_all = spread(prompt_tokens, PLANE).reshape(prompts, depth)
    image_all = spread(image_tokens, COLUMN).reshape(images, depth)
    codes = spread(code, PLANE)[:, 0, :own_prompts].reshape(1, prompts)
    bias = jnp.where(codes % 2 == 1, 0.0, MASKED).astype(F32).reshape(prompts, 1)

    image_value_wt = image_value_weight.T
    prompt_value_wt = prompt_value_weight.T
    image_out_wt = image_out_weight.T
    prompt_out_wt = prompt_out_weight.T

    head_columns = lambda n: block((n, HD), lambda h: (0, h))
    head_rows = lambda n: block((HD, n), lambda h: (h, 0))

    queries, image_values_t = pl.pallas_call(
        image_kernel,
        grid=(heads,),
        in_specs=[
            whole(image_all),
            block((1, depth), lambda h: (0, 0)),
            head_columns(depth),
            head_rows(depth),
        ],
        out_specs=[head_columns(images), head_rows(images)],
        out_shape=[shaped((images, width), BF), shaped((width, images), BF)],
        scratch_shapes=[pltpu.VMEM((images, depth), BF)],
        compiler_params=pltpu.CompilerParams(**PARAMS),
        cost_estimate=cost(4 * images * depth * width, 6 * images * width),
        name="image_projection",
    )(image_all, image_gain.reshape(1, depth), query_weight, image_value_wt)

    pair_flops = 4 * images * prompts * width
    stat_rows = heads * prompts // 128
    keys, prompt_part_t, col_lse = pl.pallas_call(
        column_kernel,
        grid=(heads,),
        in_specs=[
            whole(prompt_all),
            block((1, depth), lambda h: (0, 0)),
            head_columns(depth),
            head_columns(images),
            head_rows(images),
        ],
        out_specs=[
            head_columns(prompts),
            head_rows(prompts),
            block((stat_rows, 128), lambda h: (0, 0)),
        ],
        out_shape=[
            shaped((prompts, width), BF),
            shaped((width, prompts), F32),
            shaped((stat_rows, 128), F32),
        ],
        scratch_shapes=[pltpu.VMEM((prompts, depth), BF)],
        compiler_params=pltpu.CompilerParams(**PARAMS),
        cost_estimate=cost(pair_flops, 6 * images * width, images * prompts * heads),
        name="column_attention",
    )(prompt_all, prompt_gain.reshape(1, depth), key_weight, queries, image_values_t)

    col_lse_all = spread(col_lse, PLANE)

    row_stat_rows = heads * images // 128
    image_part_t, row_lse = pl.pallas_call(
        row_kernel,
        grid=(heads,),
        in_specs=[
            whole(prompt_all),
            block((1, depth), lambda h: (0, 0)),
            head_rows(depth),
            head_columns(prompts),
            head_columns(images),
            block((prompts, 1), lambda h: (0, 0)),
        ],
        out_specs=[
            head_rows(images),
            block((row_stat_rows, 128), lambda h: (0, 0)),
        ],
        out_shape=[
            shaped((width, images), F32),
            shaped((row_stat_rows, 128), F32),
        ],
        scratch_shapes=[pltpu.VMEM((prompts, depth), BF)],
        compiler_params=pltpu.CompilerParams(**PARAMS),
        cost_estimate=cost(pair_flops, 6 * images * width, images * prompts * heads),
        name="row_attention",
    )(prompt_all, prompt_gain.reshape(1, depth), prompt_value_wt, keys, queries, bias)

    row_lse_all = spread(row_lse, COLUMN)

    prompt_sent, category_sent = pl.pallas_call(
        prompt_out_kernel,
        out_shape=[
            shaped((prompts, depth), BF),
            shaped((planes, 2 * categories // planes, 128), BF),
        ],
        compiler_params=pltpu.CompilerParams(vmem_limit_bytes=40 * 2**20),
        cost_estimate=cost(2 * prompts * depth * (width + categories), 6 * prompts * width),
        name="prompt_projection_out",
    )(col_lse_all, col_lse, prompt_part_t, prompt_out_wt, codes)

    category_arrived = swap(category_sent, PLANE)
    prompt_arrived = swap(prompt_sent.reshape(planes, own_prompts, depth), PLANE)

    place = lax.axis_index(PLANE)
    rows = category_arrived.shape[1]
    own_category = pl.pallas_call(
        category_kernel,
        in_specs=[pl.BlockSpec(memory_space=pltpu.SMEM)]
        + [pl.BlockSpec(memory_space=pltpu.VMEM)] * 4,
        out_shape=shaped((2, rows, 128), F32),
        compiler_params=pltpu.CompilerParams(vmem_limit_bytes=40 * 2**20),
        cost_estimate=cost(2 * rows * prompts * depth, 4 * prompts * depth),
        name="category_partial",
    )(
        jnp.stack([place // 2, place % 2]).astype(jnp.int32),
        category_arrived,
        codes,
        prompt_all,
        prompt_layer_scale.reshape(1, depth),
    )
    partials = jnp.sum(spread(own_category, COLUMN), axis=0)
    means = (partials[0] / partials[1]).astype(BF)
    mean_all = spread(means, PLANE)
    category_embed = (
        mean_all.reshape(planes // 2, 2, rows, 128)
        .transpose(0, 2, 1, 3)
        .reshape(categories, depth)
        .astype(F32)
    )

    image_sent = pl.pallas_call(
        image_out_kernel,
        out_shape=shaped((images, depth), BF),
        compiler_params=pltpu.CompilerParams(vmem_limit_bytes=40 * 2**20),
        cost_estimate=cost(2 * images * depth * width, 6 * images * width),
        name="image_projection_out",
    )(row_lse_all, row_lse, image_part_t, image_out_wt)
    image_arrived = swap(image_sent.reshape(columns, own_images, depth), COLUMN)
    image_delta = jnp.sum(image_arrived.astype(F32), axis=0)
    joined_image = (image_tokens.astype(F32) + image_layer_scale * image_delta).astype(BF)

    prompt_delta = jnp.sum(prompt_arrived.astype(F32), axis=0)
    joined_prompt = (prompt_tokens.astype(F32) + prompt_layer_scale * prompt_delta).astype(BF)
    return (joined_image, joined_prompt, category_embed)


def solution(mesh):
    finer = Mesh(mesh.devices.reshape(4, 8, 2, 2, 2), ALL)
    replicated = (P(),) * 10
    return jax.shard_map(
        on_device,
        mesh=finer,
        in_specs=(P(ALL, None), P(PROMPT_ORDER, None), P(PROMPT_ORDER), P(PROMPT_ORDER), *replicated),
        out_specs=(P(ALL, None), P(PROMPT_ORDER, None), P()),
        check_vma=False,
    )
```

```python
import math

import jax
import jax.numpy as jnp
from jax import lax
from jax.experimental import pallas as pl
from jax.experimental.pallas import tpu as pltpu
from jax.sharding import Mesh
from jax.sharding import PartitionSpec as P


HD = 256
CHUNK = 256
EPSILON = 1e-05
MASKED = -1e30
ALL = ("x", "z", "yl", "yh", "c")
PROMPT_ORDER = ("yh", "c", "x", "z", "yl")
PLANE = ("x", "z")
COLUMN = ("yl", "yh", "c")
BF = jnp.bfloat16
F32 = jnp.float32


def swap(parts, axes):
    return lax.all_to_all(parts, axes, split_axis=0, concat_axis=0, tiled=True)


def normed(tokens, gain_row):
    values = tokens.astype(F32)
    centered = values - jnp.mean(values, axis=-1, keepdims=True)
    variance = jnp.mean(centered * centered, axis=-1, keepdims=True)
    return (centered * lax.rsqrt(variance + EPSILON) * gain_row).astype(BF)


def dot(left, right):
    return jnp.dot(left, right, preferred_element_type=F32)


def dot_nt(left, right):
    return lax.dot_general(left, right, (((1,), (1,)), ((), ())), preferred_element_type=F32)


def pack_kernel(tokens, ids, valid, out):
    peers, count, depth = out.shape[0], *tokens.shape
    groups = count // 8
    lane = lax.broadcasted_iota(jnp.int32, (8, 128), 1)
    token = lax.broadcasted_iota(jnp.int32, (8, count), 0)
    wanted = lax.broadcasted_iota(jnp.int32, (8, count), 1)
    code = jnp.zeros((8, 128), F32)
    for group in range(groups):
        chosen = wanted == token + 8 * group
        pick = lambda line: jnp.sum(
            jnp.where(chosen, line[...].astype(F32), 0.0), axis=1, keepdims=True
        )
        number, real = pick(ids), pick(valid)
        sixteens = jnp.floor(number * (1.0 / 16.0))
        code = jnp.where(lane == 8 * group, real, code)
        code = jnp.where(lane == 8 * group + 1, sixteens, code)
        code = jnp.where(lane == 8 * group + 2, number - 16.0 * sixteens, code)
    copied = lambda piece: jnp.broadcast_to(piece[None], (peers, *piece.shape))
    out[:, :count] = copied(tokens[:, :128])
    out[:, count : 2 * count] = copied(tokens[:, 128:])
    out[:, 2 * count :] = copied(code.astype(BF))


def tokens_of(packed):
    peers, rows, _ = packed.shape
    count = (rows - 8) // 2
    left = packed[:, :count].reshape(peers * count, 128)
    right = packed[:, count : 2 * count].reshape(peers * count, 128)
    return jnp.concatenate([left, right], axis=1)


def codes_of(packed):
    peers, rows, _ = packed.shape
    count = (rows - 8) // 2
    code = packed[:, 2 * count :].astype(F32)
    groups = [code] + [pltpu.roll(code, 128 - 8 * k, 2) for k in range(1, count // 8)]
    return jnp.concatenate(groups, axis=1).reshape(peers * count, 128)


def image_norm_kernel(place, *refs):
    *images, gain, out = refs
    for k, part in enumerate(images):
        rows = part.shape[0]
        at = pl.multiple_of((place[0] ^ k) * rows, rows)
        out[pl.ds(at, rows), :] = normed(part[...], gain[...])


def attend(reduced, kept, values_t, bias, out_t, lse, head):
    for at in range(0, kept.shape[0], CHUNK):
        scores = dot_nt(reduced, kept[at : at + CHUNK])
        if bias is not None:
            scores = scores + bias
        top = jnp.max(scores, axis=0, keepdims=True)
        weights = jnp.exp2(scores - top)
        total = jnp.sum(weights, axis=0, keepdims=True)
        numer = dot(values_t, weights.astype(BF))
        out_t[:, at : at + CHUNK] = (numer * (1.0 / total)).astype(BF)
        stat = top + jnp.log2(total)
        rows = kept.shape[0] // 128
        for k in range(CHUNK // 128):
            lse[pl.ds(head * rows + at // 128 + k, 1), :] = stat[:, k * 128 : (k + 1) * 128]


def copied_at_end(head, lse, lse_copies):
    @pl.when(head == pl.num_programs(0) - 1)
    def _():
        lse_copies[...] = jnp.broadcast_to(lse[...][None], lse_copies.shape)


def queries_of(images, query_w):
    factor = math.log2(math.e) / math.sqrt(HD)
    return (dot(images[...], query_w[...]) * factor).astype(BF)


def column_kernel(
    images, packed, gain, query_w, value_w, key_w, out_t, lse, lse_copies, held
):
    head = pl.program_id(0)

    @pl.when(head == 0)
    def _():
        held[...] = normed(tokens_of(packed), gain[...])

    values_t = dot_nt(value_w[...].T, images[...]).astype(BF)
    key = dot(held[...], key_w[...]).astype(BF)
    attend(queries_of(images, query_w), key, values_t, None, out_t, lse, head)
    copied_at_end(head, lse, lse_copies)


def row_kernel(
    images, packed, gain, query_w, key_w, value_w, out_t, lse, members, held, bias
):
    head = pl.program_id(0)

    @pl.when(head == 0)
    def _():
        held[...] = normed(tokens_of(packed), gain[...])
        codes = codes_of(packed)
        members[...] = members_of(codes, 0, members.shape[0]).astype(BF)
        bias[...] = jnp.broadcast_to(jnp.where(codes[:, :1] > 0, 0.0, MASKED), bias.shape)

    values_t = dot_nt(value_w[...].T, held[...]).astype(BF)
    key = dot(held[...], key_w[...]).astype(BF)
    attend(key, queries_of(images, query_w), values_t, bias[:, :1], out_t, lse, head)


def add_projected(share, out_t, out_w, total):
    head = pl.program_id(0)
    rows = share.shape[0] // pl.num_programs(0)
    line = jnp.concatenate([share[pl.ds(head * rows + k, 1), :] for k in range(rows)], axis=1)
    term = dot(out_w[...].T, (out_t[...] * line).astype(BF))

    @pl.when(head == 0)
    def _():
        total[...] = term

    @pl.when(head > 0)
    def _():
        total[...] += term


def image_out_kernel(place, lse_whole, lse, out_t, out_w, *refs):
    *sent, share, total, turned = refs
    head = pl.program_id(0)

    @pl.when(head == 0)
    def _():
        share[...] = jnp.exp2(lse[...] - lse_whole[...])

    add_projected(share, out_t, out_w, total)

    @pl.when(head == pl.num_programs(0) - 1)
    def _():
        turned[...] = total[...].T.astype(BF)
        for k, part in enumerate(sent):
            rows = part.shape[0]
            part[...] = turned[pl.ds(pl.multiple_of((place[0] ^ k) * rows, rows), rows), :]


def members_of(codes, first, count):
    lines = codes.T
    ids = lines[1:2] * 16.0 + lines[2:3]
    wanted = (first + lax.broadcasted_iota(jnp.int32, (count, codes.shape[0]), 0)).astype(F32)
    return jnp.where(ids == wanted, jnp.where(lines[0:1] > 0, 1.0, 0.0), 0.0)


def prompt_out_kernel(lse_all, lse, out_t, out_w, members, sent, share, total, held):
    head = pl.program_id(0)

    @pl.when(head == 0)
    def _():
        gathered = lse_all[...]
        highest = jnp.max(gathered, axis=0)
        summed = jnp.sum(jnp.exp2(gathered - highest[None]), axis=0)
        share[...] = jnp.exp2(lse[...] - highest - jnp.log2(summed))

    held[pl.ds(head * members.shape[0], members.shape[0]), :] = members[...]
    add_projected(share, out_t, out_w, total)

    @pl.when(head == pl.num_programs(0) - 1)
    def _():
        contribution = total[...].T.astype(BF)
        peers, rows, wide = sent.shape
        depth = wide - 128
        sent[:, :, :depth] = contribution.reshape(peers, rows, depth)
        sums = dot(held[...], contribution).astype(BF)
        for group in range(peers // 2):
            for side in range(2):
                sent[2 * group + side, :, depth:] = sums[
                    group * rows : (group + 1) * rows, side * 128 : (side + 1) * 128
                ]


def category_kernel(place, arrived, packed, scale, out):
    _, rows, wide = arrived.shape
    depth = wide - 128
    group, side = place[0] // 2, place[0] % 2
    members = members_of(codes_of(packed), group * rows, rows)
    base = dot(members.astype(BF), tokens_of(packed))
    own = jnp.where(side == 0, base[:, :128], base[:, 128:])
    factor = jnp.where(side == 0, scale[:, :128], scale[:, 128:])
    sums = own + factor * jnp.sum(arrived[:, :, depth:].astype(F32), axis=0)
    tally = jnp.broadcast_to(jnp.sum(members, axis=1, keepdims=True), sums.shape)
    out[:, :, :128] = jnp.broadcast_to(sums[None], (out.shape[0], rows, 128))
    out[:, :, 128:] = jnp.broadcast_to(tally[None], (out.shape[0], rows, 128))


def mean_kernel(partials, out):
    sums = jnp.sum(partials[...], axis=0)
    out[...] = jnp.broadcast_to((sums[:, :128] / sums[:, 128:]).astype(BF)[None], out.shape)


def table_kernel(pieces, out):
    rows = pieces.shape[1]
    for group in range(pieces.shape[0] // 2):
        for side in range(2):
            out[group * rows : (group + 1) * rows, side * 128 : (side + 1) * 128] = pieces[
                2 * group + side
            ].astype(F32)


def block(shape, index):
    return pl.BlockSpec(shape, index)


def whole(array):
    rank = len(array.shape)
    return pl.BlockSpec(array.shape, lambda h: (0,) * rank)


def shaped(shape, dtype):
    return jax.ShapeDtypeStruct(shape, dtype)


def far(shape, dtype):
    return pltpu.HBM(shape, dtype)


def kept_far(*arrays):
    return [pltpu.with_memory_space_constraint(a, pltpu.HBM) for a in arrays]


def cost(flops, moved, exps=0):
    return pl.CostEstimate(flops=flops, bytes_accessed=moved, transcendentals=exps)


LIMIT = 16 * 2**20


def params(**more):
    return pltpu.CompilerParams(vmem_limit_bytes=LIMIT, **more)


def on_device(
    image_tokens,
    prompt_tokens,
    category_ids,
    prompt_valid,
    image_gain,
    prompt_gain,
    query_weight,
    key_weight,
    image_value_weight,
    prompt_value_weight,
    image_out_weight,
    prompt_out_weight,
    image_layer_scale,
    prompt_layer_scale,
):
    width = query_weight.shape[1]
    heads = width // HD
    depth = image_tokens.shape[1]
    planes = lax.axis_size(PLANE)
    columns = lax.axis_size(COLUMN)
    own_prompts = prompt_tokens.shape[0]
    own_images = image_tokens.shape[0]
    images = own_images * columns
    prompts = own_prompts * planes
    categories = prompts * columns // 16

    packed = pl.pallas_call(
        pack_kernel,
        out_shape=shaped((planes, 2 * own_prompts + 8, 128), BF),
        compiler_params=params(),
        name="pack",
    )(*kept_far(prompt_tokens, category_ids.reshape(1, -1), prompt_valid.reshape(1, -1)))
    prompt_all = swap(packed, PLANE)
    image_parts = [image_tokens]
    for k in range(1, columns):
        turned = [(i, i ^ k) for i in range(columns)]
        image_parts.append(lax.ppermute(image_tokens, COLUMN, turned))

    head_columns = lambda n: block((n, HD), lambda h: (0, h))
    head_rows = lambda n: block((HD, n), lambda h: (h, 0))
    row = lambda n: block((1, n), lambda h: (0, 0))

    pair_flops = 4 * images * prompts * width
    stat_rows = heads * prompts // 128
    stats = lambda n: block((n, 128), lambda h: (0, 0))
    scalar = pl.BlockSpec(memory_space=pltpu.SMEM)
    column_place = lax.axis_index(COLUMN).astype(jnp.int32).reshape(1)
    image_row = image_gain.reshape(1, depth)
    prompt_row = prompt_gain.reshape(1, depth)
    image_normed = pl.pallas_call(
        image_norm_kernel,
        in_specs=[scalar] + [pl.BlockSpec(memory_space=pltpu.VMEM)] * (columns + 1),
        out_shape=shaped((images, depth), BF),
        compiler_params=params(),
        cost_estimate=cost(10 * images * depth, 4 * images * depth),
        name="image_norm",
    )(column_place, *kept_far(image_tokens), *image_parts[1:], *kept_far(image_row))
    prompt_part_t, col_lse, col_lse_copies = pl.pallas_call(
        column_kernel,
        grid=(heads,),
        in_specs=[
            whole(image_normed),
            whole(prompt_all),
            row(depth),
            head_columns(depth),
            head_columns(depth),
            head_columns(depth),
        ],
        out_specs=[
            head_rows(prompts),
            stats(stat_rows),
            block((planes, stat_rows, 128), lambda h: (0, 0, 0)),
        ],
        out_shape=[
            far((width, prompts), BF),
            shaped((stat_rows, 128), F32),
            shaped((planes, stat_rows, 128), F32),
        ],
        scratch_shapes=[pltpu.VMEM((prompts, depth), BF)],
        compiler_params=params(dimension_semantics=("arbitrary",)),
        cost_estimate=cost(2 * pair_flops, 6 * images * width, images * prompts * heads),
        name="column_attention",
    )(image_normed, prompt_all, *kept_far(prompt_row, query_weight, image_value_weight, key_weight))

    col_lse_all = swap(col_lse_copies, PLANE)

    row_stat_rows = heads * images // 128
    image_part_t, row_lse, members = pl.pallas_call(
        row_kernel,
        grid=(heads,),
        in_specs=[
            whole(image_normed),
            whole(prompt_all),
            row(depth),
            head_columns(depth),
            head_columns(depth),
            head_columns(depth),
        ],
        out_specs=[
            head_rows(images),
            stats(row_stat_rows),
            block((categories, prompts), lambda h: (0, 0)),
        ],
        out_shape=[
            far((width, images), BF),
            shaped((row_stat_rows, 128), F32),
            far((categories, prompts), BF),
        ],
        scratch_shapes=[pltpu.VMEM((prompts, depth), BF), pltpu.VMEM((prompts, 128), F32)],
        compiler_params=params(dimension_semantics=("arbitrary",)),
        cost_estimate=cost(2 * pair_flops, 6 * images * width, images * prompts * heads),
        name="row_attention",
    )(
        image_normed,
        prompt_all,
        *kept_far(prompt_row, query_weight, key_weight, prompt_value_weight),
    )

    row_whole = row_lse
    for bit in (1, 2, 4):
        other = lax.ppermute(row_whole, COLUMN, [(i, i ^ bit) for i in range(columns)])
        apart = jnp.exp2(-jnp.abs(row_whole - other))
        row_whole = jnp.maximum(row_whole, other) + jnp.log2(1.0 + apart)

    plane_sent = pl.pallas_call(
        prompt_out_kernel,
        grid=(heads,),
        in_specs=[
            whole(col_lse_all),
            whole(col_lse),
            head_rows(prompts),
            head_rows(depth),
            block((categories // heads, prompts), lambda h: (h, 0)),
        ],
        out_specs=block((planes, own_prompts, depth + 128), lambda h: (0, 0, 0)),
        out_shape=shaped((planes, own_prompts, depth + 128), BF),
        scratch_shapes=[
            pltpu.VMEM(col_lse.shape, F32),
            pltpu.VMEM((depth, prompts), F32),
            pltpu.VMEM((categories, prompts), BF),
        ],
        compiler_params=params(dimension_semantics=("arbitrary",)),
        cost_estimate=cost(2 * prompts * depth * (width + categories), 6 * prompts * width),
        name="prompt_projection_out",
    )(col_lse_all, col_lse, *kept_far(prompt_part_t, prompt_out_weight, members))
    plane_arrived = swap(plane_sent, PLANE)

    image_sent = pl.pallas_call(
        image_out_kernel,
        grid=(heads,),
        in_specs=[scalar, whole(row_whole), whole(row_lse), head_rows(images), head_rows(depth)],
        out_specs=[block((own_images, depth), lambda h: (0, 0))] * columns,
        out_shape=[shaped((own_images, depth), BF)] * columns,
        scratch_shapes=[
            pltpu.VMEM(row_lse.shape, F32),
            pltpu.VMEM((depth, images), F32),
            pltpu.VMEM((images, depth), BF),
        ],
        compiler_params=params(dimension_semantics=("arbitrary",)),
        cost_estimate=cost(2 * images * depth * width, 6 * images * width),
        name="image_projection_out",
    )(column_place, row_whole, row_lse, *kept_far(image_part_t, image_out_weight))

    category_copies = pl.pallas_call(
        category_kernel,
        in_specs=[scalar] + [pl.BlockSpec(memory_space=pltpu.VMEM)] * 3,
        out_shape=shaped((columns, own_prompts, depth), F32),
        compiler_params=params(),
        cost_estimate=cost(2 * own_prompts * prompts * depth, 4 * prompts * depth),
        name="category_partial",
    )(
        lax.axis_index(PLANE).astype(jnp.int32).reshape(1),
        plane_arrived,
        prompt_all,
        prompt_layer_scale.reshape(1, depth),
    )
    partials = swap(category_copies, COLUMN)
    mean_copies = pl.pallas_call(
        mean_kernel,
        out_shape=shaped((planes, own_prompts, 128), BF),
        compiler_params=params(),
        name="category_mean",
    )(partials)
    mean_all = swap(mean_copies, PLANE)
    category_embed = pl.pallas_call(
        table_kernel,
        out_shape=shaped((categories, depth), F32),
        compiler_params=params(),
        name="category_table",
    )(mean_all)

    image_delta = image_sent[0].astype(F32)
    for k in range(1, columns):
        turned = [(i, i ^ k) for i in range(columns)]
        image_delta += lax.ppermute(image_sent[k], COLUMN, turned).astype(F32)
    joined_image = (image_tokens.astype(F32) + image_layer_scale * image_delta).astype(BF)
    prompt_delta = jnp.sum(plane_arrived[:, :, :depth].astype(F32), axis=0)
    joined_prompt = (prompt_tokens.astype(F32) + prompt_layer_scale * prompt_delta).astype(BF)
    return (joined_image, joined_prompt, category_embed)


def solution(mesh):
    finer = Mesh(mesh.devices.reshape(4, 8, 2, 2, 2), ALL)
    replicated = (P(),) * 10
    return jax.shard_map(
        on_device,
        mesh=finer,
        in_specs=(P(ALL, None), P(PROMPT_ORDER, None), P(PROMPT_ORDER), P(PROMPT_ORDER), *replicated),
        out_specs=(P(ALL, None), P(PROMPT_ORDER, None), P()),
        check_vma=False,
    )
```

```python
import functools
import math

import jax
import jax.numpy as jnp
from jax import lax
from jax.experimental import pallas as pl
from jax.experimental.pallas import tpu as pltpu
from jax.sharding import Mesh
from jax.sharding import PartitionSpec as P


HD = 256
CHUNK = 256
PAIRED = 2
EPSILON = 1e-05
MASKED = -1e30
ALL = ("x", "z", "yl", "yh", "c")
PROMPT_ORDER = ("yh", "c", "x", "z", "yl")
PLANE = ("x", "z")
COLUMN = ("yl", "yh", "c")
LINE = ("yl", "yh")
CORE = "c"
BF = jnp.bfloat16
F32 = jnp.float32


def swap(parts, axes):
    return lax.all_to_all(parts, axes, split_axis=0, concat_axis=0, tiled=True)


def normed(tokens, gain_row):
    values = tokens.astype(F32)
    centered = values - jnp.mean(values, axis=-1, keepdims=True)
    variance = jnp.mean(centered * centered, axis=-1, keepdims=True)
    return (centered * lax.rsqrt(variance + EPSILON) * gain_row).astype(BF)


def dot(left, right):
    return jnp.dot(left, right, preferred_element_type=F32)


def dot_nt(left, right):
    return lax.dot_general(left, right, (((1,), (1,)), ((), ())), preferred_element_type=F32)


def pack_kernel(tokens, ids, valid, out):
    peers, count, depth = out.shape[0], *tokens.shape
    groups = count // 8
    lane = lax.broadcasted_iota(jnp.int32, (8, 128), 1)
    token = lax.broadcasted_iota(jnp.int32, (8, count), 0)
    wanted = lax.broadcasted_iota(jnp.int32, (8, count), 1)
    code = jnp.zeros((8, 128), F32)
    for group in range(groups):
        chosen = wanted == token + 8 * group
        pick = lambda line: jnp.sum(
            jnp.where(chosen, line[...].astype(F32), 0.0), axis=1, keepdims=True
        )
        number, real = pick(ids), pick(valid)
        sixteens = jnp.floor(number * (1.0 / 16.0))
        code = jnp.where(lane == 8 * group, real, code)
        code = jnp.where(lane == 8 * group + 1, sixteens, code)
        code = jnp.where(lane == 8 * group + 2, number - 16.0 * sixteens, code)
    copied = lambda piece: jnp.broadcast_to(piece[None], (peers, *piece.shape))
    out[:, :count] = copied(tokens[:, :128])
    out[:, count : 2 * count] = copied(tokens[:, 128:])
    out[:, 2 * count :] = copied(code.astype(BF))


def tokens_of(packed):
    peers, rows, _ = packed.shape
    count = (rows - 8) // 2
    left = packed[:, :count].reshape(peers * count, 128)
    right = packed[:, count : 2 * count].reshape(peers * count, 128)
    return jnp.concatenate([left, right], axis=1)


def codes_of(packed):
    peers, rows, _ = packed.shape
    count = (rows - 8) // 2
    code = packed[:, 2 * count :].astype(F32)
    groups = [code] + [pltpu.roll(code, 128 - 8 * k, 2) for k in range(1, count // 8)]
    return jnp.concatenate(groups, axis=1).reshape(peers * count, 128)


def image_norm_kernel(place, *refs):
    *images, gain, out = refs
    for k, part in enumerate(images):
        rows = part.shape[0]
        at = pl.multiple_of((place[0] ^ k) * rows, rows)
        out[pl.ds(at, rows), :] = normed(part[...], gain[...])


def attend(reduced, kept, values_t, bias, out_t, lse, head):
    rows = kept.shape[0] // 128
    starts = range(0, kept.shape[0], CHUNK)
    following = dot_nt(reduced, kept[:CHUNK])
    for at in starts:
        scores = following
        if at + CHUNK < kept.shape[0]:
            following = dot_nt(reduced, kept[at + CHUNK : at + 2 * CHUNK])
        if bias is not None:
            scores = scores + bias
        top = jnp.max(scores, axis=0, keepdims=True)
        weights = jnp.exp2(scores - top)
        total = jnp.sum(weights, axis=0, keepdims=True)
        numer = dot(values_t, weights.astype(BF))
        out_t[:, at : at + CHUNK] = (numer * (1.0 / total)).astype(BF)
        stat = top + jnp.log2(total)
        for k in range(CHUNK // 128):
            lse[pl.ds(head * rows + at // 128 + k, 1), :] = stat[:, k * 128 : (k + 1) * 128]


def copied_at_end(head, lse, lse_copies):
    @pl.when(head == pl.num_programs(0) - 1)
    def _():
        lse_copies[...] = jnp.broadcast_to(lse[...][None], lse_copies.shape)


def queries_of(images, query_w):
    factor = math.log2(math.e) / math.sqrt(HD)
    return (dot(images[...], query_w[...]) * factor).astype(BF)


def join_halves(core, own, other, held):
    rows = own.shape[0]
    held[pl.ds(pl.multiple_of(core[0] * rows, rows), rows), :] = own[...]
    held[pl.ds(pl.multiple_of((1 - core[0]) * rows, rows), rows), :] = other[...]


def column_kernel(
    core, own, other, packed, gain, query_w, value_w, key_w, out_t, lse, lse_copies, images, held
):
    head = pl.program_id(0)

    @pl.when(head == 0)
    def _():
        join_halves(core, own, other, images)
        held[...] = normed(tokens_of(packed), gain[...])

    values_t = dot_nt(value_w[...].T, images[...]).astype(BF)
    key = dot(held[...], key_w[...]).astype(BF)
    attend(queries_of(images, query_w), key, values_t, None, out_t, lse, head)
    copied_at_end(head, lse, lse_copies)


def row_kernel(
    core, own, other, packed, gain, query_w, key_w, value_w, out_t, lse, members, images, held, bias
):
    head = pl.program_id(0)

    @pl.when(head == 0)
    def _():
        join_halves(core, own, other, images)
        held[...] = normed(tokens_of(packed), gain[...])
        codes = codes_of(packed)
        members[...] = members_of(codes, 0, members.shape[0]).astype(BF)
        bias[...] = jnp.broadcast_to(jnp.where(codes[:, :1] > 0, 0.0, MASKED), bias.shape)

    values_t = dot_nt(value_w[...].T, held[...]).astype(BF)
    key = dot(held[...], key_w[...]).astype(BF)
    attend(key, queries_of(images, query_w), values_t, bias[:, :1], out_t, lse, head)


def add_projected(share, out_t, out_w, total):
    step = pl.program_id(0)
    group = out_t.shape[0] // HD
    rows = share.shape[0] // (pl.num_programs(0) * group)
    term = None
    for k in range(group):
        at = (step * group + k) * rows
        line = jnp.concatenate([share[pl.ds(at + r, 1), :] for r in range(rows)], axis=1)
        block = slice(k * HD, (k + 1) * HD)
        part = dot(out_w[block, :].T, (out_t[block, :] * line).astype(BF))
        term = part if term is None else term + part

    @pl.when(step == 0)
    def _():
        total[...] = term

    @pl.when(step > 0)
    def _():
        total[...] += term


def image_out_kernel(core, lse_whole, lse, out_t, out_w, own, other, share, total, turned):
    head = pl.program_id(0)

    @pl.when(head == 0)
    def _():
        share[...] = jnp.exp2(lse[...] - lse_whole[...])

    add_projected(share, out_t, out_w, total)

    @pl.when(head == pl.num_programs(0) - 1)
    def _():
        turned[...] = total[...].T.astype(BF)
        rows = own.shape[0]
        own[...] = turned[pl.ds(pl.multiple_of(core[0] * rows, rows), rows), :]
        other[...] = turned[pl.ds(pl.multiple_of((1 - core[0]) * rows, rows), rows), :]


def image_sum_kernel(place, own, arrived, *sent):
    for k, part in enumerate(sent):
        rows = part.shape[0]
        at = pl.ds(pl.multiple_of((place[0] ^ k) * rows, rows), rows)
        part[...] = (own[at, :].astype(F32) + arrived[at, :].astype(F32)).astype(BF)


def members_of(codes, first, count):
    lines = codes.T
    ids = lines[1:2] * 16.0 + lines[2:3]
    wanted = (first + lax.broadcasted_iota(jnp.int32, (count, codes.shape[0]), 0)).astype(F32)
    return jnp.where(ids == wanted, jnp.where(lines[0:1] > 0, 1.0, 0.0), 0.0)


def prompt_out_kernel(lse_all, lse, out_t, out_w, members, sent, share, total, held):
    head = pl.program_id(0)

    @pl.when(head == 0)
    def _():
        gathered = lse_all[...]
        highest = jnp.max(gathered, axis=0)
        summed = jnp.sum(jnp.exp2(gathered - highest[None]), axis=0)
        share[...] = jnp.exp2(lse[...] - highest - jnp.log2(summed))

    held[pl.ds(head * members.shape[0], members.shape[0]), :] = members[...]
    add_projected(share, out_t, out_w, total)

    @pl.when(head == pl.num_programs(0) - 1)
    def _():
        contribution = total[...].T.astype(BF)
        peers, rows, wide = sent.shape
        depth = wide - 128
        sent[:, :, :depth] = contribution.reshape(peers, rows, depth)
        sums = dot(held[...], contribution).astype(BF)
        for group in range(peers // 2):
            for side in range(2):
                sent[2 * group + side, :, depth:] = sums[
                    group * rows : (group + 1) * rows, side * 128 : (side + 1) * 128
                ]


def category_kernel(place, arrived, packed, scale, out):
    _, rows, wide = arrived.shape
    depth = wide - 128
    group, side = place[0] // 2, place[0] % 2
    members = members_of(codes_of(packed), group * rows, rows)
    base = dot(members.astype(BF), tokens_of(packed))
    own = jnp.where(side == 0, base[:, :128], base[:, 128:])
    factor = jnp.where(side == 0, scale[:, :128], scale[:, 128:])
    sums = own + factor * jnp.sum(arrived[:, :, depth:].astype(F32), axis=0)
    tally = jnp.broadcast_to(jnp.sum(members, axis=1, keepdims=True), sums.shape)
    out[:, :, :128] = jnp.broadcast_to(sums[None], (out.shape[0], rows, 128))
    out[:, :, 128:] = jnp.broadcast_to(tally[None], (out.shape[0], rows, 128))


def mean_kernel(partials, out):
    sums = jnp.sum(partials[...], axis=0)
    out[...] = jnp.broadcast_to((sums[:, :128] / sums[:, 128:]).astype(BF)[None], out.shape)


def table_kernel(pieces, out):
    rows = pieces.shape[1]
    for group in range(pieces.shape[0] // 2):
        for side in range(2):
            out[group * rows : (group + 1) * rows, side * 128 : (side + 1) * 128] = pieces[
                2 * group + side
            ].astype(F32)


def block(shape, index):
    return pl.BlockSpec(shape, index)


def whole(array):
    rank = len(array.shape)
    return pl.BlockSpec(array.shape, lambda h: (0,) * rank)


def shaped(shape, dtype):
    return jax.ShapeDtypeStruct(shape, dtype)


def far(shape, dtype):
    return pltpu.HBM(shape, dtype)


def kept_far(*arrays):
    return [pltpu.with_memory_space_constraint(a, pltpu.HBM) for a in arrays]


def cost(flops, moved, exps=0):
    return pl.CostEstimate(flops=flops, bytes_accessed=moved, transcendentals=exps)


LIMIT = 16 * 2**20


def params(**more):
    return pltpu.CompilerParams(vmem_limit_bytes=LIMIT, **more)


def on_device(
    image_tokens,
    prompt_tokens,
    category_ids,
    prompt_valid,
    image_gain,
    prompt_gain,
    query_weight,
    key_weight,
    image_value_weight,
    prompt_value_weight,
    image_out_weight,
    prompt_out_weight,
    image_layer_scale,
    prompt_layer_scale,
):
    width = query_weight.shape[1]
    heads = width // HD
    depth = image_tokens.shape[1]
    planes = lax.axis_size(PLANE)
    columns = lax.axis_size(COLUMN)
    own_prompts = prompt_tokens.shape[0]
    own_images = image_tokens.shape[0]
    images = own_images * columns
    prompts = own_prompts * planes
    categories = prompts * columns // 16

    packed = pl.pallas_call(
        pack_kernel,
        out_shape=shaped((planes, 2 * own_prompts + 8, 128), BF),
        compiler_params=params(),
        name="pack",
    )(*kept_far(prompt_tokens, category_ids.reshape(1, -1), prompt_valid.reshape(1, -1)))
    prompt_all = swap(packed, PLANE)
    line = lax.axis_size(LINE)
    half = images // 2
    swapped = [(0, 1), (1, 0)]
    image_parts = [image_tokens]
    for k in range(1, line):
        image_parts.append(lax.ppermute(image_tokens, LINE, [(i, i ^ k) for i in range(line)]))

    head_columns = lambda n: block((n, HD), lambda h: (0, h))
    head_rows = lambda n: block((HD, n), lambda h: (h, 0))
    pair_rows = lambda n: block((PAIRED * HD, n), lambda h: (h, 0))
    row = lambda n: block((1, n), lambda h: (0, 0))

    pair_flops = 4 * images * prompts * width
    stat_rows = heads * prompts // 128
    stats = lambda n: block((n, 128), lambda h: (0, 0))
    scalar = pl.BlockSpec(memory_space=pltpu.SMEM)
    line_place = lax.axis_index(LINE).astype(jnp.int32).reshape(1)
    core = lax.axis_index(CORE).astype(jnp.int32).reshape(1)
    image_row = image_gain.reshape(1, depth)
    prompt_row = prompt_gain.reshape(1, depth)
    image_own = pl.pallas_call(
        image_norm_kernel,
        in_specs=[scalar] + [pl.BlockSpec(memory_space=pltpu.VMEM)] * (line + 1),
        out_shape=shaped((half, depth), BF),
        compiler_params=params(),
        cost_estimate=cost(10 * half * depth, 4 * half * depth),
        name="image_norm",
    )(line_place, *kept_far(image_tokens), *image_parts[1:], *kept_far(image_row))
    image_other = lax.ppermute(image_own, CORE, swapped)
    prompt_part_t, col_lse, col_lse_copies = pl.pallas_call(
        column_kernel,
        grid=(heads,),
        in_specs=[
            scalar,
            whole(image_own),
            whole(image_other),
            whole(prompt_all),
            row(depth),
            head_columns(depth),
            head_columns(depth),
            head_columns(depth),
        ],
        out_specs=[
            head_rows(prompts),
            stats(stat_rows),
            block((planes, stat_rows, 128), lambda h: (0, 0, 0)),
        ],
        out_shape=[
            far((width, prompts), BF),
            shaped((stat_rows, 128), F32),
            shaped((planes, stat_rows, 128), F32),
        ],
        scratch_shapes=[pltpu.VMEM((images, depth), BF), pltpu.VMEM((prompts, depth), BF)],
        compiler_params=params(dimension_semantics=("arbitrary",)),
        cost_estimate=cost(2 * pair_flops, 6 * images * width, images * prompts * heads),
        name="column_attention",
    )(
        core,
        image_own,
        image_other,
        prompt_all,
        *kept_far(prompt_row, query_weight, image_value_weight, key_weight),
    )

    col_lse_all = swap(col_lse_copies, PLANE)

    row_stat_rows = heads * images // 128
    image_part_t, row_lse, members = pl.pallas_call(
        row_kernel,
        grid=(heads,),
        in_specs=[
            scalar,
            whole(image_own),
            whole(image_other),
            whole(prompt_all),
            row(depth),
            head_columns(depth),
            head_columns(depth),
            head_columns(depth),
        ],
        out_specs=[
            head_rows(images),
            stats(row_stat_rows),
            block((categories, prompts), lambda h: (0, 0)),
        ],
        out_shape=[
            far((width, images), BF),
            shaped((row_stat_rows, 128), F32),
            far((categories, prompts), BF),
        ],
        scratch_shapes=[
            pltpu.VMEM((images, depth), BF),
            pltpu.VMEM((prompts, depth), BF),
            pltpu.VMEM((prompts, 128), F32),
        ],
        compiler_params=params(dimension_semantics=("arbitrary",)),
        cost_estimate=cost(2 * pair_flops, 6 * images * width, images * prompts * heads),
        name="row_attention",
    )(
        core,
        image_own,
        image_other,
        prompt_all,
        *kept_far(prompt_row, query_weight, key_weight, prompt_value_weight),
    )

    def mixed(parts):
        top = functools.reduce(jnp.maximum, parts)
        return top + jnp.log2(sum(jnp.exp2(part - top) for part in parts))

    row_parts = [row_lse]
    for k in range(1, line):
        row_parts.append(lax.ppermute(row_lse, LINE, [(i, i ^ k) for i in range(line)]))
    row_own = mixed(row_parts)
    row_whole = mixed([row_own, lax.ppermute(row_own, CORE, swapped)])

    plane_sent = pl.pallas_call(
        prompt_out_kernel,
        grid=(heads // PAIRED,),
        in_specs=[
            whole(col_lse_all),
            whole(col_lse),
            pair_rows(prompts),
            pair_rows(depth),
            block((categories * PAIRED // heads, prompts), lambda h: (h, 0)),
        ],
        out_specs=block((planes, own_prompts, depth + 128), lambda h: (0, 0, 0)),
        out_shape=shaped((planes, own_prompts, depth + 128), BF),
        scratch_shapes=[
            pltpu.VMEM(col_lse.shape, F32),
            pltpu.VMEM((depth, prompts), F32),
            pltpu.VMEM((categories, prompts), BF),
        ],
        compiler_params=params(dimension_semantics=("arbitrary",)),
        cost_estimate=cost(2 * prompts * depth * (width + categories), 6 * prompts * width),
        name="prompt_projection_out",
    )(col_lse_all, col_lse, *kept_far(prompt_part_t, prompt_out_weight, members))
    plane_arrived = swap(plane_sent, PLANE)

    own_sum, other_sum = pl.pallas_call(
        image_out_kernel,
        grid=(heads // PAIRED,),
        in_specs=[scalar, whole(row_whole), whole(row_lse), pair_rows(images), pair_rows(depth)],
        out_specs=[block((half, depth), lambda h: (0, 0))] * 2,
        out_shape=[shaped((half, depth), BF)] * 2,
        scratch_shapes=[
            pltpu.VMEM(row_lse.shape, F32),
            pltpu.VMEM((depth, images), F32),
            pltpu.VMEM((images, depth), BF),
        ],
        compiler_params=params(dimension_semantics=("arbitrary",)),
        cost_estimate=cost(2 * images * depth * width, 6 * images * width),
        name="image_projection_out",
    )(core, row_whole, row_lse, *kept_far(image_part_t, image_out_weight))

    category_copies = pl.pallas_call(
        category_kernel,
        in_specs=[scalar] + [pl.BlockSpec(memory_space=pltpu.VMEM)] * 3,
        out_shape=shaped((columns, own_prompts, depth), F32),
        compiler_params=params(),
        cost_estimate=cost(2 * own_prompts * prompts * depth, 4 * prompts * depth),
        name="category_partial",
    )(
        lax.axis_index(PLANE).astype(jnp.int32).reshape(1),
        plane_arrived,
        prompt_all,
        prompt_layer_scale.reshape(1, depth),
    )
    partials = swap(category_copies, COLUMN)
    mean_copies = pl.pallas_call(
        mean_kernel,
        out_shape=shaped((planes, own_prompts, 128), BF),
        compiler_params=params(),
        name="category_mean",
    )(partials)
    mean_all = swap(mean_copies, PLANE)
    category_embed = pl.pallas_call(
        table_kernel,
        out_shape=shaped((categories, depth), F32),
        compiler_params=params(),
        name="category_table",
    )(mean_all)

    crossed_sum = lax.ppermute(other_sum, CORE, swapped)
    image_sent = pl.pallas_call(
        image_sum_kernel,
        in_specs=[scalar] + [pl.BlockSpec(memory_space=pltpu.VMEM)] * 2,
        out_shape=[shaped((own_images, depth), BF)] * line,
        compiler_params=params(),
        cost_estimate=cost(half * depth, 6 * half * depth),
        name="image_sum",
    )(line_place, own_sum, crossed_sum)
    image_delta = image_sent[0].astype(F32)
    for k in range(1, line):
        turned = [(i, i ^ k) for i in range(line)]
        image_delta += lax.ppermute(image_sent[k], LINE, turned).astype(F32)
    joined_image = (image_tokens.astype(F32) + image_layer_scale * image_delta).astype(BF)
    prompt_delta = jnp.sum(plane_arrived[:, :, :depth].astype(F32), axis=0)
    joined_prompt = (prompt_tokens.astype(F32) + prompt_layer_scale * prompt_delta).astype(BF)
    return (joined_image, joined_prompt, category_embed)


def solution(mesh):
    finer = Mesh(mesh.devices.reshape(4, 8, 2, 2, 2), ALL)
    replicated = (P(),) * 10
    return jax.shard_map(
        on_device,
        mesh=finer,
        in_specs=(P(ALL, None), P(PROMPT_ORDER, None), P(PROMPT_ORDER), P(PROMPT_ORDER), *replicated),
        out_specs=(P(ALL, None), P(PROMPT_ORDER, None), P()),
        check_vma=False,
    )
```

```python
import functools
import math

import jax
import jax.numpy as jnp
from jax import lax
from jax.experimental import pallas as pl
from jax.experimental.pallas import tpu as pltpu
from jax.sharding import Mesh
from jax.sharding import PartitionSpec as P


HD = 256
CHUNK = 256
PAIRED = 2
EPSILON = 1e-05
MASKED = -1e30
ALL = ("x", "z", "yl", "yh", "c")
PROMPT_ORDER = ("yh", "c", "x", "z", "yl")
PLANE = ("x", "z")
COLUMN = ("yl", "yh", "c")
LINE = ("yl", "yh")
CORE = "c"
BF = jnp.bfloat16
F32 = jnp.float32


def swap(parts, axes):
    return lax.all_to_all(parts, axes, split_axis=0, concat_axis=0, tiled=True)


def normed(tokens, gain_row):
    values = tokens.astype(F32)
    centered = values - jnp.mean(values, axis=-1, keepdims=True)
    variance = jnp.mean(centered * centered, axis=-1, keepdims=True)
    return (centered * lax.rsqrt(variance + EPSILON) * gain_row).astype(BF)


def dot(left, right):
    return jnp.dot(left, right, preferred_element_type=F32)


def dot_nt(left, right):
    return lax.dot_general(left, right, (((1,), (1,)), ((), ())), preferred_element_type=F32)


def pack_kernel(tokens, ids, valid, out):
    peers, count, depth = out.shape[0], *tokens.shape
    groups = count // 8
    lane = lax.broadcasted_iota(jnp.int32, (8, 128), 1)
    token = lax.broadcasted_iota(jnp.int32, (8, count), 0)
    wanted = lax.broadcasted_iota(jnp.int32, (8, count), 1)
    code = jnp.zeros((8, 128), F32)
    for group in range(groups):
        chosen = wanted == token + 8 * group
        pick = lambda line: jnp.sum(
            jnp.where(chosen, line[...].astype(F32), 0.0), axis=1, keepdims=True
        )
        number, real = pick(ids), pick(valid)
        sixteens = jnp.floor(number * (1.0 / 16.0))
        code = jnp.where(lane == 8 * group, real, code)
        code = jnp.where(lane == 8 * group + 1, sixteens, code)
        code = jnp.where(lane == 8 * group + 2, number - 16.0 * sixteens, code)
    copied = lambda piece: jnp.broadcast_to(piece[None], (peers, *piece.shape))
    out[:, :count] = copied(tokens[:, :128])
    out[:, count : 2 * count] = copied(tokens[:, 128:])
    out[:, 2 * count :] = copied(code.astype(BF))


def tokens_of(packed):
    peers, rows, _ = packed.shape
    count = (rows - 8) // 2
    left = packed[:, :count].reshape(peers * count, 128)
    right = packed[:, count : 2 * count].reshape(peers * count, 128)
    return jnp.concatenate([left, right], axis=1)


def codes_of(packed):
    peers, rows, _ = packed.shape
    count = (rows - 8) // 2
    code = packed[:, 2 * count :].astype(F32)
    groups = [code] + [pltpu.roll(code, 128 - 8 * k, 2) for k in range(1, count // 8)]
    return jnp.concatenate(groups, axis=1).reshape(peers * count, 128)


def image_norm_kernel(place, *refs):
    *images, gain, out = refs
    for k, part in enumerate(images):
        rows = part.shape[0]
        at = pl.multiple_of((place[0] ^ k) * rows, rows)
        out[pl.ds(at, rows), :] = normed(part[...], gain[...])


def attend(reduced, kept, values_t, bias, out_t, lse, head):
    rows = kept.shape[0] // 128
    starts = range(0, kept.shape[0], CHUNK)
    following = dot_nt(reduced, kept[:CHUNK])
    for at in starts:
        scores = following
        if at + CHUNK < kept.shape[0]:
            following = dot_nt(reduced, kept[at + CHUNK : at + 2 * CHUNK])
        if bias is not None:
            scores = scores + bias
        top = jnp.max(scores, axis=0, keepdims=True)
        weights = jnp.exp2(scores - top)
        total = jnp.sum(weights, axis=0, keepdims=True)
        numer = dot(values_t, weights.astype(BF))
        out_t[:, at : at + CHUNK] = (numer * (1.0 / total)).astype(BF)
        stat = top + jnp.log2(total)
        for k in range(CHUNK // 128):
            lse[pl.ds(head * rows + at // 128 + k, 1), :] = stat[:, k * 128 : (k + 1) * 128]


def copied_at_end(head, lse, lse_copies):
    @pl.when(head == pl.num_programs(0) - 1)
    def _():
        lse_copies[...] = jnp.broadcast_to(lse[...][None], lse_copies.shape)


def queries_of(images, query_w):
    factor = math.log2(math.e) / math.sqrt(HD)
    return (dot(images[...], query_w[...]) * factor).astype(BF)


def join_halves(core, own, other, held):
    rows = own.shape[0]
    held[pl.ds(pl.multiple_of(core[0] * rows, rows), rows), :] = own[...]
    held[pl.ds(pl.multiple_of((1 - core[0]) * rows, rows), rows), :] = other[...]


def column_kernel(
    core, own, other, packed, gain, query_w, value_w, key_w, out_t, lse, lse_copies, images, held
):
    head = pl.program_id(0)

    @pl.when(head == 0)
    def _():
        join_halves(core, own, other, images)
        held[...] = normed(tokens_of(packed), gain[...])

    values_t = dot_nt(value_w[...].T, images[...]).astype(BF)
    key = dot(held[...], key_w[...]).astype(BF)
    attend(queries_of(images, query_w), key, values_t, None, out_t, lse, head)
    copied_at_end(head, lse, lse_copies)


def row_kernel(
    core, own, other, packed, gain, query_w, key_w, value_w, out_t, lse, members, images, held, bias
):
    head = pl.program_id(0)

    @pl.when(head == 0)
    def _():
        join_halves(core, own, other, images)
        held[...] = normed(tokens_of(packed), gain[...])
        codes = codes_of(packed)
        members[...] = members_of(codes, 0, members.shape[0]).astype(BF)
        bias[...] = jnp.broadcast_to(jnp.where(codes[:, :1] > 0, 0.0, MASKED), bias.shape)

    values_t = dot_nt(value_w[...].T, held[...]).astype(BF)
    key = dot(held[...], key_w[...]).astype(BF)
    attend(key, queries_of(images, query_w), values_t, bias[:, :1], out_t, lse, head)


def add_projected(share, out_t, out_w, total):
    step = pl.program_id(0)
    group = out_t.shape[0] // HD
    rows = share.shape[0] // (pl.num_programs(0) * group)
    term = None
    for k in range(group):
        at = (step * group + k) * rows
        line = jnp.concatenate([share[pl.ds(at + r, 1), :] for r in range(rows)], axis=1)
        block = slice(k * HD, (k + 1) * HD)
        part = dot(out_w[block, :].T, (out_t[block, :] * line).astype(BF))
        term = part if term is None else term + part

    @pl.when(step == 0)
    def _():
        total[...] = term

    @pl.when(step > 0)
    def _():
        total[...] += term


def image_out_kernel(core, lse_whole, lse, out_t, out_w, own, other, share, total, turned):
    head = pl.program_id(0)

    @pl.when(head == 0)
    def _():
        share[...] = jnp.exp2(lse[...] - lse_whole[...])

    add_projected(share, out_t, out_w, total)

    @pl.when(head == pl.num_programs(0) - 1)
    def _():
        turned[...] = total[...].T.astype(BF)
        rows = own.shape[0]
        own[...] = turned[pl.ds(pl.multiple_of(core[0] * rows, rows), rows), :]
        other[...] = turned[pl.ds(pl.multiple_of((1 - core[0]) * rows, rows), rows), :]


def image_sum_kernel(place, own, arrived, *sent):
    for k, part in enumerate(sent):
        rows = part.shape[0]
        at = pl.ds(pl.multiple_of((place[0] ^ k) * rows, rows), rows)
        part[...] = (own[at, :].astype(F32) + arrived[at, :].astype(F32)).astype(BF)


def members_of(codes, first, count):
    lines = codes.T
    ids = lines[1:2] * 16.0 + lines[2:3]
    wanted = (first + lax.broadcasted_iota(jnp.int32, (count, codes.shape[0]), 0)).astype(F32)
    return jnp.where(ids == wanted, jnp.where(lines[0:1] > 0, 1.0, 0.0), 0.0)


def prompt_out_kernel(lse_all, lse, out_t, out_w, members, sent, share, total, held):
    head = pl.program_id(0)

    @pl.when(head == 0)
    def _():
        gathered = lse_all[...]
        highest = jnp.max(gathered, axis=0)
        summed = jnp.sum(jnp.exp2(gathered - highest[None]), axis=0)
        share[...] = jnp.exp2(lse[...] - highest - jnp.log2(summed))

    held[pl.ds(head * members.shape[0], members.shape[0]), :] = members[...]
    add_projected(share, out_t, out_w, total)

    @pl.when(head == pl.num_programs(0) - 1)
    def _():
        contribution = total[...].T.astype(BF)
        peers, rows, wide = sent.shape
        depth = wide - 128
        sent[:, :, :depth] = contribution.reshape(peers, rows, depth)
        sums = dot(held[...], contribution).astype(BF)
        for group in range(peers // 2):
            for side in range(2):
                sent[2 * group + side, :, depth:] = sums[
                    group * rows : (group + 1) * rows, side * 128 : (side + 1) * 128
                ]


def base_kernel(place, packed, base, tally):
    rows = base.shape[0]
    group, side = place[0] // 2, place[0] % 2
    members = members_of(codes_of(packed), group * rows, rows)
    wide = dot(members.astype(BF), tokens_of(packed))
    base[...] = jnp.where(side == 0, wide[:, :128], wide[:, 128:])
    tally[...] = jnp.broadcast_to(jnp.sum(members, axis=1, keepdims=True), tally.shape)


def category_kernel(place, arrived, base, tally, scale, out):
    wide = arrived.shape[2]
    factor = jnp.where(place[0] % 2 == 0, scale[:, :128], scale[:, 128:])
    out[:, :128] = base[...] + factor * jnp.sum(arrived[:, :, wide - 128 :].astype(F32), axis=0)
    out[:, 128:] = tally[...]


def mean_kernel(*refs):
    *parts, out = refs
    sums = sum(part[...] for part in parts)
    out[...] = jnp.broadcast_to((sums[:, :128] / sums[:, 128:]).astype(BF)[None], out.shape)


def table_kernel(pieces, out):
    rows = pieces.shape[1]
    for group in range(pieces.shape[0] // 2):
        for side in range(2):
            out[group * rows : (group + 1) * rows, side * 128 : (side + 1) * 128] = pieces[
                2 * group + side
            ].astype(F32)


def block(shape, index):
    return pl.BlockSpec(shape, index)


def whole(array):
    rank = len(array.shape)
    return pl.BlockSpec(array.shape, lambda h: (0,) * rank)


def shaped(shape, dtype):
    return jax.ShapeDtypeStruct(shape, dtype)


def far(shape, dtype):
    return pltpu.HBM(shape, dtype)


def kept_far(*arrays):
    return [pltpu.with_memory_space_constraint(a, pltpu.HBM) for a in arrays]


def cost(flops, moved, exps=0):
    return pl.CostEstimate(flops=flops, bytes_accessed=moved, transcendentals=exps)


LIMIT = 16 * 2**20


def params(**more):
    return pltpu.CompilerParams(vmem_limit_bytes=LIMIT, **more)


def on_device(
    image_tokens,
    prompt_tokens,
    category_ids,
    prompt_valid,
    image_gain,
    prompt_gain,
    query_weight,
    key_weight,
    image_value_weight,
    prompt_value_weight,
    image_out_weight,
    prompt_out_weight,
    image_layer_scale,
    prompt_layer_scale,
):
    width = query_weight.shape[1]
    heads = width // HD
    depth = image_tokens.shape[1]
    planes = lax.axis_size(PLANE)
    columns = lax.axis_size(COLUMN)
    own_prompts = prompt_tokens.shape[0]
    own_images = image_tokens.shape[0]
    images = own_images * columns
    prompts = own_prompts * planes
    categories = prompts * columns // 16

    packed = pl.pallas_call(
        pack_kernel,
        out_shape=shaped((planes, 2 * own_prompts + 8, 128), BF),
        compiler_params=params(),
        name="pack",
    )(*kept_far(prompt_tokens, category_ids.reshape(1, -1), prompt_valid.reshape(1, -1)))
    prompt_all = swap(packed, PLANE)
    line = lax.axis_size(LINE)
    half = images // 2
    swapped = [(0, 1), (1, 0)]
    image_parts = [image_tokens]
    for k in range(1, line):
        image_parts.append(lax.ppermute(image_tokens, LINE, [(i, i ^ k) for i in range(line)]))

    head_columns = lambda n: block((n, HD), lambda h: (0, h))
    head_rows = lambda n: block((HD, n), lambda h: (h, 0))
    pair_rows = lambda n: block((PAIRED * HD, n), lambda h: (h, 0))
    row = lambda n: block((1, n), lambda h: (0, 0))

    pair_flops = 4 * images * prompts * width
    stat_rows = heads * prompts // 128
    stats = lambda n: block((n, 128), lambda h: (0, 0))
    scalar = pl.BlockSpec(memory_space=pltpu.SMEM)
    line_place = lax.axis_index(LINE).astype(jnp.int32).reshape(1)
    core = lax.axis_index(CORE).astype(jnp.int32).reshape(1)
    image_row = image_gain.reshape(1, depth)
    prompt_row = prompt_gain.reshape(1, depth)
    image_own = pl.pallas_call(
        image_norm_kernel,
        in_specs=[scalar] + [pl.BlockSpec(memory_space=pltpu.VMEM)] * (line + 1),
        out_shape=shaped((half, depth), BF),
        compiler_params=params(),
        cost_estimate=cost(10 * half * depth, 4 * half * depth),
        name="image_norm",
    )(line_place, *kept_far(image_tokens), *image_parts[1:], *kept_far(image_row))
    image_other = lax.ppermute(image_own, CORE, swapped)
    prompt_part_t, col_lse, col_lse_copies = pl.pallas_call(
        column_kernel,
        grid=(heads,),
        in_specs=[
            scalar,
            whole(image_own),
            whole(image_other),
            whole(prompt_all),
            row(depth),
            head_columns(depth),
            head_columns(depth),
            head_columns(depth),
        ],
        out_specs=[
            head_rows(prompts),
            stats(stat_rows),
            block((planes, stat_rows, 128), lambda h: (0, 0, 0)),
        ],
        out_shape=[
            far((width, prompts), BF),
            shaped((stat_rows, 128), F32),
            shaped((planes, stat_rows, 128), F32),
        ],
        scratch_shapes=[pltpu.VMEM((images, depth), BF), pltpu.VMEM((prompts, depth), BF)],
        compiler_params=params(dimension_semantics=("arbitrary",)),
        cost_estimate=cost(2 * pair_flops, 6 * images * width, images * prompts * heads),
        name="column_attention",
    )(
        core,
        image_own,
        image_other,
        prompt_all,
        *kept_far(prompt_row, query_weight, image_value_weight, key_weight),
    )

    col_lse_all = swap(col_lse_copies, PLANE)

    row_stat_rows = heads * images // 128
    image_part_t, row_lse, members = pl.pallas_call(
        row_kernel,
        grid=(heads,),
        in_specs=[
            scalar,
            whole(image_own),
            whole(image_other),
            whole(prompt_all),
            row(depth),
            head_columns(depth),
            head_columns(depth),
            head_columns(depth),
        ],
        out_specs=[
            head_rows(images),
            stats(row_stat_rows),
            block((categories, prompts), lambda h: (0, 0)),
        ],
        out_shape=[
            far((width, images), BF),
            shaped((row_stat_rows, 128), F32),
            far((categories, prompts), BF),
        ],
        scratch_shapes=[
            pltpu.VMEM((images, depth), BF),
            pltpu.VMEM((prompts, depth), BF),
            pltpu.VMEM((prompts, 128), F32),
        ],
        compiler_params=params(dimension_semantics=("arbitrary",)),
        cost_estimate=cost(2 * pair_flops, 6 * images * width, images * prompts * heads),
        name="row_attention",
    )(
        core,
        image_own,
        image_other,
        prompt_all,
        *kept_far(prompt_row, query_weight, key_weight, prompt_value_weight),
    )

    def mixed(parts):
        top = functools.reduce(jnp.maximum, parts)
        return top + jnp.log2(sum(jnp.exp2(part - top) for part in parts))

    row_parts = [row_lse]
    for k in range(1, line):
        row_parts.append(lax.ppermute(row_lse, LINE, [(i, i ^ k) for i in range(line)]))
    row_own = mixed(row_parts)
    row_whole = mixed([row_own, lax.ppermute(row_own, CORE, swapped)])

    plane_sent = pl.pallas_call(
        prompt_out_kernel,
        grid=(heads // PAIRED,),
        in_specs=[
            whole(col_lse_all),
            whole(col_lse),
            pair_rows(prompts),
            pair_rows(depth),
            block((categories * PAIRED // heads, prompts), lambda h: (h, 0)),
        ],
        out_specs=block((planes, own_prompts, depth + 128), lambda h: (0, 0, 0)),
        out_shape=shaped((planes, own_prompts, depth + 128), BF),
        scratch_shapes=[
            pltpu.VMEM(col_lse.shape, F32),
            pltpu.VMEM((depth, prompts), F32),
            pltpu.VMEM((categories, prompts), BF),
        ],
        compiler_params=params(dimension_semantics=("arbitrary",)),
        cost_estimate=cost(2 * prompts * depth * (width + categories), 6 * prompts * width),
        name="prompt_projection_out",
    )(col_lse_all, col_lse, *kept_far(prompt_part_t, prompt_out_weight, members))
    plane_arrived = swap(plane_sent, PLANE)

    own_sum, other_sum = pl.pallas_call(
        image_out_kernel,
        grid=(heads // PAIRED,),
        in_specs=[scalar, whole(row_whole), whole(row_lse), pair_rows(images), pair_rows(depth)],
        out_specs=[block((half, depth), lambda h: (0, 0))] * 2,
        out_shape=[shaped((half, depth), BF)] * 2,
        scratch_shapes=[
            pltpu.VMEM(row_lse.shape, F32),
            pltpu.VMEM((depth, images), F32),
            pltpu.VMEM((images, depth), BF),
        ],
        compiler_params=params(dimension_semantics=("arbitrary",)),
        cost_estimate=cost(2 * images * depth * width, 6 * images * width),
        name="image_projection_out",
    )(core, row_whole, row_lse, *kept_far(image_part_t, image_out_weight))

    plane_place = lax.axis_index(PLANE).astype(jnp.int32).reshape(1)
    base, tally = pl.pallas_call(
        base_kernel,
        in_specs=[scalar, pl.BlockSpec(memory_space=pltpu.VMEM)],
        out_shape=[shaped((own_prompts, 128), F32)] * 2,
        compiler_params=params(),
        cost_estimate=cost(2 * own_prompts * prompts * depth, 4 * prompts * depth),
        name="category_base",
    )(plane_place, prompt_all)
    category_own = pl.pallas_call(
        category_kernel,
        in_specs=[scalar] + [pl.BlockSpec(memory_space=pltpu.VMEM)] * 4,
        out_shape=shaped((own_prompts, depth), F32),
        compiler_params=params(),
        cost_estimate=cost(2 * own_prompts * prompts * depth, 4 * prompts * depth),
        name="category_partial",
    )(
        plane_place,
        plane_arrived,
        base,
        tally,
        prompt_layer_scale.reshape(1, depth),
    )
    core_sum = category_own + lax.ppermute(category_own, CORE, swapped)
    line_sums = [core_sum]
    for k in range(1, line):
        line_sums.append(lax.ppermute(core_sum, LINE, [(i, i ^ k) for i in range(line)]))
    mean_copies = pl.pallas_call(
        mean_kernel,
        out_shape=shaped((planes, own_prompts, 128), BF),
        compiler_params=params(),
        name="category_mean",
    )(*line_sums)
    mean_all = swap(mean_copies, PLANE)
    category_embed = pl.pallas_call(
        table_kernel,
        out_shape=shaped((categories, depth), F32),
        compiler_params=params(),
        name="category_table",
    )(mean_all)

    crossed_sum = lax.ppermute(other_sum, CORE, swapped)
    image_sent = pl.pallas_call(
        image_sum_kernel,
        in_specs=[scalar] + [pl.BlockSpec(memory_space=pltpu.VMEM)] * 2,
        out_shape=[shaped((own_images, depth), BF)] * line,
        compiler_params=params(),
        cost_estimate=cost(half * depth, 6 * half * depth),
        name="image_sum",
    )(line_place, own_sum, crossed_sum)
    image_delta = image_sent[0].astype(F32)
    for k in range(1, line):
        turned = [(i, i ^ k) for i in range(line)]
        image_delta += lax.ppermute(image_sent[k], LINE, turned).astype(F32)
    joined_image = (image_tokens.astype(F32) + image_layer_scale * image_delta).astype(BF)
    prompt_delta = jnp.sum(plane_arrived[:, :, :depth].astype(F32), axis=0)
    joined_prompt = (prompt_tokens.astype(F32) + prompt_layer_scale * prompt_delta).astype(BF)
    return (joined_image, joined_prompt, category_embed)


def solution(mesh):
    finer = Mesh(mesh.devices.reshape(4, 8, 2, 2, 2), ALL)
    replicated = (P(),) * 10
    return jax.shard_map(
        on_device,
        mesh=finer,
        in_specs=(P(ALL, None), P(PROMPT_ORDER, None), P(PROMPT_ORDER), P(PROMPT_ORDER), *replicated),
        out_specs=(P(ALL, None), P(PROMPT_ORDER, None), P()),
        check_vma=False,
    )
```
